32 devices in a mesh: men: 16 (over z, x, core), women: 2 (over y).
Axes of the slice: x: 2, y: 2, z: 4, core: 2. Of those that a mesh axis runs over, the one named last changes fastest.
Arguments:
- men_traits: bfloat16 [64, 16384], P(None, ('men', 'women')), may hold values from -4 to 4
- women_traits: bfloat16 [64, 8192], P(None, ('women', 'men')), may hold values from -4 to 4
- affinity: float32 [64, 64], replicated, may hold values from -0.375 to 0.375
- observed: float32 [64, 64], replicated, may hold values from -0.25 to 0.25
- men_mass: float32 [16384], P('men'), may hold values from 0.5 to 2
- women_mass: float32 [8192], P('women'), may hold values from 0.5 to 2
Outputs:
- men_scale: float32 [16384], P('men')
- women_scale: float32 [8192], P('women')
- updated: float32 [64, 64], replicated
The draws below stay inside these ranges and needn't reach their ends.
All inputs are finite; a program needn't handle non-finite values.
Results may differ from the reference program's by a relative error of at most 0.0022.
Values may be sent and summed in bfloat16 or wider, within the bound.
A program may use at most 64 MiB of HBM per device.

```python
import math
import jax
import jax.numpy as jnp
from jax import lax

K = 64
M_DEV = 1024
W_DEV = 4096
ITERS = 2
NM = 16384
NW = 8192


def men_levels(key):
    block_count = NM // M_DEV
    return jax.random.uniform(jax.random.fold_in(key, 101), (K, block_count), jnp.float32, -1.0, 0.6)


def trait_noise(key, columns):
    return jax.random.truncated_normal(key, -2.9, 2.9, (K, columns), jnp.float32)


def draw_men_traits(key, part):
    levels = men_levels(key)
    spread_levels = jnp.repeat(levels, M_DEV, axis=1, total_repeat_length=NM)
    noise = trait_noise(jax.random.fold_in(key, 102), NM)
    values = jnp.clip(spread_levels + noise, -4.0, 4.0)
    return values.astype(jnp.bfloat16)


def draw_men_mass(key, part):
    levels = men_levels(key)
    block_log = 0.5 * (levels[0] + 0.2) / 0.8
    spread_log = jnp.repeat(block_log, M_DEV, total_repeat_length=NM)
    noise = jax.random.uniform(jax.random.fold_in(key, 103), (NM,), jnp.float32, -0.18, 0.18)
    values = jnp.clip(jnp.exp(spread_log + noise), 0.5, 2.0)
    return values.astype(jnp.float32)


def draw_women_traits(key, part):
    block_count = NW // W_DEV
    levels = jax.random.uniform(jax.random.fold_in(key, 201), (K, block_count), jnp.float32, -0.4, 0.8)
    spread_levels = jnp.repeat(levels, W_DEV, axis=1, total_repeat_length=NW)
    noise = trait_noise(jax.random.fold_in(key, 202), NW)
    values = jnp.clip(spread_levels + noise, -4.0, 4.0)
    return values.astype(jnp.bfloat16)


def level_of(rng, dims, split, least, top_value):
    loudness, own = 1.0, jax.random.fold_in(rng, 6)
    for dim, parts in split:
        steps = jnp.exp(jax.random.uniform(jax.random.fold_in(own, dim), (parts,), jnp.float32, least / len(split), top_value / len(split)))
        loudness = loudness * jnp.repeat(steps, dims[dim] // parts).reshape([-1 if axis == dim else 1 for axis in range(len(dims))])
    return loudness


def bell_draw(rng, shape, scale, reach, held_as=jnp.bfloat16):
    drawn = jax.random.normal(rng, shape, jnp.float32) * scale
    return jnp.minimum(jnp.maximum(drawn, -reach), reach).astype(held_as)


def setup_inputs(seed: int = 0) -> dict:
    splits = jax.random.split(jax.random.key(seed), 7)
    return {
        "men_traits": draw_men_traits(jax.random.fold_in(splits[6], 71), 0),
        "women_traits": draw_women_traits(jax.random.fold_in(splits[6], 71), 0),
        "affinity": bell_draw(splits[2], (K, K), 0.025, 0.375, jnp.float32),
        "observed": bell_draw(splits[3], (K, K), 0.015625, 0.25, jnp.float32),
        "men_mass": draw_men_mass(jax.random.fold_in(splits[6], 71), 0),
        "women_mass": jnp.clip(jnp.exp(math.log(2.0) - 1.3862944 * jax.random.uniform(splits[5], (NW,), jnp.float32) ** level_of(splits[5], (NW,), ((0, 2),), -0.2, 0.2)), 0.5, 2.0),
    }


HIGH = lax.Precision.HIGHEST


def kernel_rows(scaled_block, women_traits, women_count):
    surplus = lax.dot_general(scaled_block, women_traits, (((0,), (0,)), ((), ())), preferred_element_type=jnp.float32)
    return jnp.exp(surplus) / women_count


def reference(men_traits, women_traits, affinity, observed, men_mass, women_mass):
    traits = men_traits.shape[0]
    men_total = men_traits.shape[1]
    women_total = women_traits.shape[1]
    women_count = float(women_total)
    block_rows = math.gcd(men_total, 1024)
    block_count = men_total // block_rows
    men_float = men_traits.astype(jnp.float32)
    scaled = jnp.dot(affinity.T, men_float, precision=HIGH).astype(jnp.bfloat16)
    scaled_blocks = scaled.reshape(traits, block_count, block_rows).transpose(1, 0, 2)
    men_blocks = men_float.reshape(traits, block_count, block_rows).transpose(1, 0, 2)
    women_float = women_traits.astype(jnp.float32)

    def rows_of(women_scale):
        def one_block(scaled_block):
            return jnp.dot(kernel_rows(scaled_block, women_traits, women_count), women_scale, precision=HIGH)
        return lax.map(one_block, scaled_blocks).reshape(men_total)

    def cols_of(men_scale):
        scale_blocks = men_scale.reshape(block_count, block_rows)

        def one_block(total, pieces):
            kernel = kernel_rows(pieces[0], women_traits, women_count)
            return total + jnp.dot(pieces[1], kernel, precision=HIGH), None
        total, _ = lax.scan(one_block, jnp.zeros((women_total,), jnp.float32), (scaled_blocks, scale_blocks))
        return total

    women_scale = jnp.ones((women_total,), jnp.float32)
    men_scale = men_mass
    for round_index in range(ITERS):
        men_scale = men_mass / rows_of(women_scale)
        women_scale = women_mass / cols_of(men_scale)

    scale_blocks = men_scale.reshape(block_count, block_rows)

    def moment_block(total, pieces):
        kernel = kernel_rows(pieces[0], women_traits, women_count)
        plan = pieces[1][:, None] * kernel * women_scale[None, :]
        inner = jnp.dot(plan, women_float.T, precision=HIGH)
        return total + jnp.dot(pieces[2], inner, precision=HIGH), None

    moment, _ = lax.scan(moment_block, jnp.zeros((traits, traits), jnp.float32), (scaled_blocks, scale_blocks, men_blocks))
    updated = affinity + observed - moment / float(men_total)
    return men_scale, women_scale, updated
```

```python
import functools
import math
import jax
import jax.numpy as jnp
from jax import lax
from jax.experimental import pallas as pl
from jax.experimental.pallas import tpu as pltpu
from jax.sharding import PartitionSpec as P

F32, BF16 = jnp.float32, jnp.bfloat16
MESH = pl.DeviceIdType.MESH
LHS_T = (((0,), (0,)), ((), ()))
RHS_T = (((1,), (1,)), ((), ()))


def split3(value):
    high = value.astype(BF16)
    rest = value - high.astype(F32)
    mid = rest.astype(BF16)
    low = (rest - mid.astype(F32)).astype(BF16)
    return high, mid, low


def factors(men):
    cores = 2 if men % 2 == 0 else 1
    chips = men // cores
    planes = 1 << (chips.bit_length() // 2)
    if chips % planes:
        planes = 1
    return planes, chips // planes, cores


def body(dims, women_axis, men_total, women_total,
         men_ref, women_ref, aff_ref, obs_ref, mm_ref, wm_ref,
         ms_out, ws_out, up_out,
         men_buf, wom_buf, scaled_ref, e_ref, t_ref, col_ref, r_buf, a_buf, z_buf,
         my_buf, ma_buf, mz_buf,
         own_sem, gy_s, gy_r, gz_s, gz_r, gx_s, gx_r, gc_s, gc_r,
         ry_s, ry_r, ca_s, ca_r, cz_s, cz_r):
    zs, xs, cs = dims
    ws = women_axis
    n = zs * xs * cs
    traits, wb = women_ref.shape
    rows = mm_ref.shape[1]
    log_count = math.log(women_total)
    mi = lax.axis_index("men")
    yi = lax.axis_index("women")
    ci = lax.rem(mi, cs)
    xi = lax.rem(lax.div(mi, cs), xs)
    zi = lax.div(mi, cs * xs)

    def men_at(z, x, c):
        return (z * xs + x) * cs + c

    def plus(value, step, size):
        return lax.rem(value + step, size)

    plane = [(dc, dx) for dc in range(cs) for dx in range(xs) if (dc, dx) != (0, 0)]
    plane_ids = [(men_at(zi, plus(xi, dx, xs), plus(ci, dc, cs)), yi) for dc, dx in plane]
    z_ids = [(men_at(plus(zi, dz, zs), xi, ci), yi) for dz in range(1, zs)]
    y_ids = [(mi, plus(yi, dy, ws)) for dy in range(1, ws)]

    own = pltpu.make_async_copy(women_ref, wom_buf.at[ci, xi, zi], own_sem)
    own.start()
    barrier = pltpu.get_barrier_semaphore()
    everyone = plane_ids + z_ids + y_ids
    for peer in everyone:
        pl.semaphore_signal(barrier, inc=1, device_id=peer, device_id_type=MESH)
    pl.semaphore_wait(barrier, len(everyone))

    def remote(src, dst, send, recv, peer):
        return pltpu.make_async_remote_copy(
            src_ref=src, dst_ref=dst, send_sem=send, recv_sem=recv,
            device_id=peer, device_id_type=MESH)

    def z_copy(dz):
        return remote(women_ref, wom_buf.at[ci, xi, zi], gz_s.at[dz], gz_r.at[dz],
                      (men_at(plus(zi, dz, zs), xi, ci), yi))

    def block_of(dx, dz):
        return wom_buf.at[ci, plus(xi, xs - dx, xs), plus(zi, zs - dz, zs)]

    def x_copy(dx, dz):
        held = block_of(0, dz)
        return remote(held, held, gx_s.at[dx, dz], gx_r.at[dx, dz],
                      (men_at(zi, plus(xi, dx, xs), ci), yi))

    def c_copy(dx, dz):
        held = block_of(dx, dz)
        return remote(held, held, gc_s.at[dx, dz], gc_r.at[dx, dz],
                      (men_at(zi, xi, plus(ci, 1, cs)), yi))

    def forward(dz):
        for dx in range(1, xs):
            x_copy(dx, dz).start()
        if cs > 1:
            c_copy(0, dz).start()

    men_copies = []
    for dy, peer in enumerate(y_ids):
        copy = remote(men_ref, men_buf.at[yi], gy_s.at[dy], gy_r.at[dy], peer)
        copy.start()
        men_copies.append(copy)
    for dz in range(1, zs):
        z_copy(dz).start()
    own.wait()
    forward(0)
    men_buf[yi] = men_ref[...]
    for copy in men_copies:
        copy.wait_recv()

    men_full = jnp.concatenate([men_buf[y] for y in range(ws)], axis=1)
    high, mid, low = [
        lax.dot_general(men_full, part, LHS_T, preferred_element_type=F32)
        for part in split3(aff_ref[...])
    ]
    scaled_ref[...] = ((low + mid) + high).astype(BF16)
    ones = jnp.ones((16, wb), BF16)
    tile = math.gcd(rows, 256)

    def fill(t, total):
        dz = lax.rem(t, zs)
        dx = lax.rem(lax.div(t, zs), xs)
        dc = lax.div(t, zs * xs)

        @pl.when((t > 0) & (t < zs))
        def _():
            z_copy(dz).wait_recv()
            forward(dz)

        if xs > 1:
            @pl.when((t >= zs) & (t < zs * xs))
            def _():
                x_copy(dx, dz).wait_recv()
                if cs > 1:
                    c_copy(dx, dz).start()

        if cs > 1:
            @pl.when(t >= zs * xs)
            def _():
                c_copy(dx, dz).wait_recv()

        bc = plus(ci, dc, cs)
        bx = plus(xi, xs - dx, xs)
        bz = plus(zi, zs - dz, zs)
        q = (bc * xs + bx) * zs + bz
        block = wom_buf[bc, bx, bz]
        for start in range(0, rows, tile):
            surplus = jnp.dot(scaled_ref[start:start + tile, :], block, preferred_element_type=F32)
            e_ref[q, start:start + tile, :] = jnp.exp(surplus - log_count).astype(BF16)
        return total + lax.dot_general(ones, e_ref[q], RHS_T, preferred_element_type=F32)

    pending = []

    def group_sum(value, buf, me, send, recv, peers):
        if not peers:
            return value
        buf[me] = value
        copies = []
        for k, peer in enumerate(peers):
            copy = remote(buf.at[me], buf.at[me], send.at[k], recv.at[k], peer)
            copy.start()
            copies.append(copy)
        for copy in copies:
            copy.wait_recv()
        pending.extend(copies)
        total = buf[0]
        for slot in range(1, buf.shape[0]):
            total = total + buf[slot]
        return total

    def men_update(it, row_sum):
        total = group_sum(row_sum, r_buf.at[it], yi, ry_s.at[it], ry_r.at[it], y_ids)
        return mm_ref[...] / total

    order = [((z * xs + x) * cs + c) for c in range(cs) for x in range(xs) for z in range(zs)]
    mass_q = jnp.concatenate([wm_ref[:, p * wb:(p + 1) * wb] for p in order], axis=0)
    plane_me = ci * xs + xi

    def women_update(it, partial):
        total = group_sum(partial, a_buf.at[it], plane_me, ca_s.at[it], ca_r.at[it], plane_ids)
        total = group_sum(total, z_buf.at[it], zi, cz_s.at[it], cz_r.at[it], z_ids)
        return mass_q / total

    zeros13 = jnp.zeros((13, rows), BF16)
    zeros13w = jnp.zeros((13, wb), BF16)

    total = lax.fori_loop(0, n, fill, jnp.zeros((16, rows), F32))
    scale = men_update(0, total[0:1, :])

    def sweep(step, carry):
        if n <= 16:
            for q in range(n):
                carry = step(q, carry)
            return carry
        return lax.fori_loop(0, n, step, carry)

    left0 = jnp.concatenate(list(split3(scale)) + [zeros13], axis=0)

    def col_step(q, carry):
        out = jnp.dot(left0, e_ref[q], preferred_element_type=F32)
        col_ref[pl.ds(q, 1), :] = out[0:1] + out[1:2] + out[2:3]
        return carry

    sweep(col_step, 0)
    col_ref[...] = women_update(0, col_ref[...])

    def row_step(q, total):
        lines = jnp.concatenate(list(split3(col_ref[pl.ds(q, 1), :])) + [zeros13w], axis=0)
        return total + lax.dot_general(lines, e_ref[q], RHS_T, preferred_element_type=F32)

    total = sweep(row_step, jnp.zeros((16, rows), F32))
    scale = men_update(1, total[0:1] + total[1:2] + total[2:3])
    ms_out[...] = scale

    weighted = (men_full.astype(F32) * scale).astype(BF16)
    left = jnp.concatenate([weighted] + list(split3(scale)) + [zeros13], axis=0)

    def both_step(q, carry):
        out = jnp.dot(left, e_ref[q], preferred_element_type=F32)
        t_ref[q] = out[0:traits]
        col_ref[pl.ds(q, 1), :] = (out[traits:traits + 1] + out[traits + 1:traits + 2]
                                   + out[traits + 2:traits + 3])
        return carry

    sweep(both_step, 0)
    women_scale = women_update(1, col_ref[...])
    col_ref[...] = women_scale
    for q, p in enumerate(order):
        ws_out[:, p * wb:(p + 1) * wb] = women_scale[q:q + 1, :]

    def moment_step(q, moment):
        c, x, z = q // (xs * zs), (q // zs) % xs, q % zs
        inner = t_ref[q] * col_ref[pl.ds(q, 1), :]
        high = inner.astype(BF16)
        low = (inner - high.astype(F32)).astype(BF16)
        both = jnp.concatenate([high, low], axis=0)
        return moment + lax.dot_general(both, wom_buf[c, x, z], RHS_T, preferred_element_type=F32)

    moment = sweep(moment_step, jnp.zeros((2 * traits, traits), F32))
    moment = moment[0:traits] + moment[traits:]
    half = traits // 2
    packed = jnp.concatenate([moment[0:half], moment[half:]], axis=1)
    packed = group_sum(packed, my_buf, yi, ry_s.at[2], ry_r.at[2], y_ids)
    packed = group_sum(packed, ma_buf, plane_me, ca_s.at[2], ca_r.at[2], plane_ids)
    packed = group_sum(packed, mz_buf, zi, cz_s.at[2], cz_r.at[2], z_ids)
    moment = jnp.concatenate([packed[:, 0:traits], packed[:, traits:]], axis=0)
    up_out[...] = aff_ref[...] + obs_ref[...] - moment * (1.0 / men_total)

    for copy in men_copies + pending:
        copy.wait_send()
    for dz in range(1, zs):
        z_copy(dz).wait_send()
    for dz in range(zs):
        for dx in range(1, xs):
            x_copy(dx, dz).wait_send()
        if cs > 1:
            for dx in range(xs):
                c_copy(dx, dz).wait_send()


def solution(mesh):
    men_axis, women_axis = mesh.shape["men"], mesh.shape["women"]
    dims = factors(men_axis)
    zs, xs, cs = dims

    def on_device(men_traits, women_traits, affinity, observed, men_mass, women_mass):
        traits, mb = men_traits.shape
        wb = women_traits.shape[1]
        rows, cols = men_mass.shape[0], women_mass.shape[0]
        n, group = men_axis, xs * cs
        dma = pltpu.SemaphoreType.DMA
        vmem = pl.BlockSpec(memory_space=pltpu.VMEM)
        half = traits // 2

        def at_least(k):
            return max(k, 1)

        out = pl.pallas_call(
            functools.partial(body, dims, women_axis, rows * men_axis, cols * women_axis),
            out_shape=(
                jax.ShapeDtypeStruct((1, rows), F32),
                jax.ShapeDtypeStruct((1, cols), F32),
                jax.ShapeDtypeStruct((traits, traits), F32),
            ),
            in_specs=[vmem] * 6,
            out_specs=(vmem, vmem, vmem),
            scratch_shapes=[
                pltpu.VMEM((women_axis, traits, mb), BF16),
                pltpu.VMEM((cs, xs, zs, traits, wb), BF16),
                pltpu.VMEM((rows, traits), BF16),
                pltpu.VMEM((n, rows, wb), BF16),
                pltpu.VMEM((n, traits, wb), F32),
                pltpu.VMEM((n, wb), F32),
                pltpu.VMEM((2, women_axis, 1, rows), F32),
                pltpu.VMEM((2, group, n, wb), F32),
                pltpu.VMEM((2, zs, n, wb), F32),
                pltpu.VMEM((women_axis, half, 2 * traits), F32),
                pltpu.VMEM((group, half, 2 * traits), F32),
                pltpu.VMEM((zs, half, 2 * traits), F32),
                dma(()),
                dma((women_axis,)), dma((women_axis,)),
                dma((zs,)), dma((zs,)),
                dma((xs, zs)), dma((xs, zs)),
                dma((xs, zs)), dma((xs, zs)),
                dma((3, women_axis)), dma((3, women_axis)),
                dma((3, group)), dma((3, group)),
                dma((3, zs)), dma((3, zs)),
            ],
            compiler_params=pltpu.CompilerParams(
                collective_id=0, has_side_effects=True, vmem_limit_bytes=60 * 1024 * 1024),
        )(men_traits, women_traits, affinity, observed,
          men_mass.reshape(1, rows), women_mass.reshape(1, cols))
        return out[0].reshape(rows), out[1].reshape(cols), out[2]

    placed = (P(None, ("men", "women")), P(None, ("women", "men")), P(), P(), P("men"), P("women"))
    return jax.shard_map(
        on_device,
        mesh=mesh,
        in_specs=placed,
        out_specs=(P("men"), P("women"), P()),
        check_vma=False,
    )
```

```python
import functools
import math
import jax
import jax.numpy as jnp
from jax import lax
from jax.experimental import pallas as pl
from jax.experimental.pallas import tpu as pltpu
from jax.sharding import PartitionSpec as P

F32, BF16 = jnp.float32, jnp.bfloat16
MESH = pl.DeviceIdType.MESH
LHS_T = (((0,), (0,)), ((), ()))
RHS_T = (((1,), (1,)), ((), ()))


def split3(value):
    high = value.astype(BF16)
    rest = value - high.astype(F32)
    mid = rest.astype(BF16)
    low = (rest - mid.astype(F32)).astype(BF16)
    return high, mid, low


def factors(men):
    cores = 2 if men % 2 == 0 else 1
    chips = men // cores
    planes = 1 << (chips.bit_length() // 2)
    if chips % planes:
        planes = 1
    return planes, chips // planes, cores


def body(dims, ws, men_total, women_total,
         men_ref, women_ref, aff_hbm, obs_hbm, mm_hbm, wm_hbm,
         ms_out, ws_out, up_out,
         men_buf, wom_buf, scaled_ref, e_ref, t_ref, col_ref, rsum_ref, scale_ref,
         aff_ref, obs_ref, wm_ref, mass_buf, wx_buf,
         r_buf, c_buf, mxy_buf, mc_buf, mz_buf,
         own_sem, gm_s, gm_r, gz_s, gz_r, gc_s, gc_r, mm_s, mm_r, wx_s, wx_r,
         rx_s, rx_r, cz_s, cz_r, mc_s, mc_r, mz_s, mz_r):
    zs, xs, cs = dims
    nm, nb = xs * ws, zs * cs
    traits, wb = women_ref.shape
    mb = men_ref.shape[1]
    rows = mm_hbm.shape[1]
    group_rows = nm * mb
    log_count = math.log(women_total)
    mi = lax.axis_index("men")
    yi = lax.axis_index("women")
    ci = lax.rem(mi, cs)
    xi = lax.rem(lax.div(mi, cs), xs)
    zi = lax.div(mi, cs * xs)
    xy_me = xi * ws + yi
    zc_me = ci * zs + zi

    def plus(value, step, size):
        return lax.rem(value + step, size)

    def xy_peer(dx, dy):
        return ((zi * xs + plus(xi, dx, xs)) * cs + ci, plus(yi, dy, ws))

    def zc_peer(dc, dz):
        return ((plus(zi, dz, zs) * xs + xi) * cs + plus(ci, dc, cs), yi)

    xy_ids = [xy_peer(dx, dy) for dx in range(xs) for dy in range(ws) if dx + dy]
    zc_ids = [zc_peer(dc, dz) for dc in range(cs) for dz in range(zs) if dc + dz]
    x_ids = [xy_peer(dx, 0) for dx in range(1, xs)]
    c_ids = [zc_peer(dc, 0) for dc in range(1, cs)]
    z_ids = [zc_peer(0, dz) for dz in range(1, zs)]

    barrier = pltpu.get_barrier_semaphore()
    everyone = xy_ids + zc_ids
    for peer in everyone:
        pl.semaphore_signal(barrier, inc=1, device_id=peer, device_id_type=MESH)
    local = [
        pltpu.make_async_copy(src, dst, own_sem.at[k])
        for k, (src, dst) in enumerate([
            (men_ref, men_buf.at[xy_me]), (women_ref, wom_buf.at[zc_me]), (aff_hbm, aff_ref),
            (mm_hbm, mass_buf.at[xi]), (wm_hbm, wm_ref), (obs_hbm, obs_ref)])
    ]
    for copy in local:
        copy.start()
    pl.semaphore_wait(barrier, len(everyone))

    def remote(src, dst, send, recv, peer):
        return pltpu.make_async_remote_copy(
            src_ref=src, dst_ref=dst, send_sem=send, recv_sem=recv,
            device_id=peer, device_id_type=MESH)

    def z_copy(dz):
        return remote(women_ref, wom_buf.at[zc_me], gz_s.at[dz], gz_r.at[dz], zc_peer(0, dz))

    def c_copy(dz):
        held = wom_buf.at[ci * zs + plus(zi, zs - dz, zs)]
        return remote(held, held, gc_s.at[dz], gc_r.at[dz], zc_peer(1, 0))

    def m_copy(k):
        return remote(men_ref, men_buf.at[xy_me], gm_s.at[k], gm_r.at[k],
                      xy_peer(lax.div(k, ws), lax.rem(k, ws)))

    for dz in range(1, zs):
        z_copy(dz).start()
    for k in range(1, nm):
        m_copy(k).start()
    pending = []
    for k, peer in enumerate(x_ids):
        copy = remote(mm_hbm, mass_buf.at[xi], mm_s.at[k], mm_r.at[k], peer)
        copy.start()
        pending.append(copy)
    mass_copies = list(pending)
    for copy in local:
        copy.wait()
    if cs > 1:
        c_copy(0).start()

    def shard_of(k):
        return plus(xi, xs - lax.div(k, ws), xs) * ws + plus(yi, ws - lax.rem(k, ws), ws)

    def rows_of(shard):
        return pl.ds(pl.multiple_of(shard * mb, mb), mb)

    def make_scaled(shard):
        high, mid, low = [
            lax.dot_general(men_buf[shard], part, LHS_T, preferred_element_type=F32)
            for part in split3(aff_ref[...])
        ]
        scaled_ref[rows_of(shard), :] = ((low + mid) + high).astype(BF16)

    make_scaled(xy_me)
    tile = math.gcd(mb, 256)
    fold = wb // 128 if wb % 128 == 0 else 1
    lanes = wb // fold
    rsum_ref[...] = jnp.zeros_like(rsum_ref)

    def fill(q, start, count):
        block = wom_buf[q]
        for part in range(count):
            at = pl.ds(pl.multiple_of(start + part * tile, tile), tile)
            surplus = jnp.dot(scaled_ref[at, :], block, preferred_element_type=F32)
            kernel = jnp.exp(surplus - log_count)
            e_ref[q, at, :] = kernel.astype(BF16)
            total = rsum_ref[at, :]
            for piece in range(fold):
                total = total + kernel[:, piece * lanes:(piece + 1) * lanes]
            rsum_ref[at, :] = total

    def z_block(dz):
        return ci * zs + plus(zi, zs - dz, zs)

    fill(zc_me, xy_me * mb, mb // tile)

    def own_men(dz, carry):
        z_copy(dz).wait_recv()
        if cs > 1:
            c_copy(dz).start()
        fill(z_block(dz), xy_me * mb, mb // tile)
        return carry

    def other_men(k, carry):
        m_copy(k).wait_recv()
        shard = shard_of(k)
        make_scaled(shard)
        for z in range(zs):
            fill(ci * zs + z, shard * mb, mb // tile)
        return carry

    def other_core(dz, carry):
        c_copy(dz).wait_recv()
        fill(plus(ci, 1, cs) * zs + plus(zi, zs - dz, zs), 0, group_rows // tile)
        return carry

    lax.fori_loop(1, zs, own_men, 0)
    lax.fori_loop(1, nm, other_men, 0)
    if cs > 1:
        lax.fori_loop(0, zs, other_core, 0)

    def group_sum(value, buf, me, send, recv, peers):
        if not peers:
            return value
        buf[me] = value
        copies = []
        for k, peer in enumerate(peers):
            copy = remote(buf.at[me], buf.at[me], send.at[k], recv.at[k], peer)
            copy.start()
            copies.append(copy)
        for copy in copies:
            copy.wait_recv()
        pending.extend(copies)
        total = buf[0]
        for slot in range(1, buf.shape[0]):
            total = total + buf[slot]
        return total

    for copy in mass_copies:
        copy.wait_recv()
    men_mass = jnp.concatenate([mass_buf[x] for x in range(xs)], axis=1)
    men_full = jnp.concatenate([men_buf[k] for k in range(nm)], axis=1)
    mass_q = None
    for x in range(xs):
        order = [(z * xs + x) * cs + c for c in range(cs) for z in range(zs)]
        mine = jnp.concatenate([wm_ref[:, p * wb:(p + 1) * wb] for p in order], axis=0)
        mass_q = mine if mass_q is None else jnp.where(xi == x, mine, mass_q)

    def men_update(it, row_sum):
        return men_mass / group_sum(row_sum, r_buf.at[it], xy_me, rx_s.at[it], rx_r.at[it], xy_ids)

    def women_update(it, partial):
        return mass_q / group_sum(partial, c_buf.at[it], zc_me, cz_s.at[it], cz_r.at[it], zc_ids)

    zeros13 = jnp.zeros((13, group_rows), BF16)
    zeros13w = jnp.zeros((13, wb), BF16)

    def sweep(step, carry):
        for q in range(nb):
            carry = step(q, carry)
        return carry

    sums = rsum_ref[...]
    high = sums.astype(BF16)
    low = (sums - high.astype(F32)).astype(BF16)
    total = lax.dot_general(jnp.ones((16, 2 * lanes), BF16), jnp.concatenate([high, low], axis=1),
                            RHS_T, preferred_element_type=F32)
    scale = men_update(0, total[0:1])
    left0 = jnp.concatenate(list(split3(scale)) + [zeros13], axis=0)

    def col_step(q, carry):
        out = jnp.dot(left0, e_ref[q], preferred_element_type=F32)
        col_ref[q:q + 1, :] = out[0:1] + out[1:2] + out[2:3]
        return carry

    sweep(col_step, 0)
    col_ref[...] = women_update(0, col_ref[...])

    def row_step(q, total):
        lines = jnp.concatenate(list(split3(col_ref[q:q + 1, :])) + [zeros13w], axis=0)
        return total + lax.dot_general(lines, e_ref[q], RHS_T, preferred_element_type=F32)

    total = sweep(row_step, jnp.zeros((16, group_rows), F32))
    scale = men_update(1, total[0:1] + total[1:2] + total[2:3])
    for x in range(xs):
        scale_ref[x] = scale[:, x * rows:(x + 1) * rows]
    ms_out[...] = scale_ref[xi]

    weighted = (men_full.astype(F32) * scale).astype(BF16)
    left = jnp.concatenate([weighted] + list(split3(scale)) + [zeros13], axis=0)

    def both_step(q, carry):
        out = jnp.dot(left, e_ref[q], preferred_element_type=F32)
        t_ref[q] = out[0:traits]
        col_ref[q:q + 1, :] = (out[traits:traits + 1] + out[traits + 1:traits + 2]
                               + out[traits + 2:traits + 3])
        return carry

    sweep(both_step, 0)
    women_scale = women_update(1, col_ref[...])
    col_ref[...] = women_scale
    wx_buf[xi] = women_scale
    wx_copies = []
    for k, peer in enumerate(x_ids):
        copy = remote(wx_buf.at[xi], wx_buf.at[xi], wx_s.at[k], wx_r.at[k], peer)
        copy.start()
        wx_copies.append(copy)
    pending.extend(wx_copies)

    def moment_step(q, moment):
        inner = t_ref[q] * col_ref[q:q + 1, :]
        high = inner.astype(BF16)
        low = (inner - high.astype(F32)).astype(BF16)
        both = jnp.concatenate([high, low], axis=0)
        return moment + lax.dot_general(both, wom_buf[q], RHS_T, preferred_element_type=F32)

    moment = sweep(moment_step, jnp.zeros((2 * traits, traits), F32))
    moment = moment[0:traits] + moment[traits:]
    half = traits // 2
    packed = jnp.concatenate([moment[0:half], moment[half:]], axis=1)
    packed = group_sum(packed, mxy_buf, xy_me, rx_s.at[2], rx_r.at[2], xy_ids)
    packed = group_sum(packed, mc_buf, ci, mc_s, mc_r, c_ids)
    for copy in wx_copies:
        copy.wait_recv()
    for x in range(xs):
        scales = wx_buf[x]
        for q in range(nb):
            p = ((q % zs) * xs + x) * cs + q // zs
            ws_out[:, p * wb:(p + 1) * wb] = scales[q:q + 1, :]
    packed = group_sum(packed, mz_buf, zi, mz_s, mz_r, z_ids)
    moment = jnp.concatenate([packed[:, 0:traits], packed[:, traits:]], axis=0)
    up_out[...] = aff_ref[...] + obs_ref[...] - moment * (1.0 / men_total)

    for copy in pending:
        copy.wait_send()
    for dz in range(1, zs):
        z_copy(dz).wait_send()
    for k in range(1, nm):
        m_copy(k).wait_send()
    if cs > 1:
        for dz in range(zs):
            c_copy(dz).wait_send()


def solution(mesh):
    men_axis, women_axis = mesh.shape["men"], mesh.shape["women"]
    dims = factors(men_axis)
    zs, xs, cs = dims

    def on_device(men_traits, women_traits, affinity, observed, men_mass, women_mass):
        traits, mb = men_traits.shape
        wb = women_traits.shape[1]
        rows, cols = men_mass.shape[0], women_mass.shape[0]
        nm, nb = xs * women_axis, zs * cs
        dma = pltpu.SemaphoreType.DMA
        vmem = pl.BlockSpec(memory_space=pltpu.VMEM)
        anywhere = pl.BlockSpec(memory_space=pl.ANY)
        packed = (traits // 2, 2 * traits)
        out = pl.pallas_call(
            functools.partial(body, dims, women_axis, rows * men_axis, cols * women_axis),
            out_shape=(
                jax.ShapeDtypeStruct((1, rows), F32),
                jax.ShapeDtypeStruct((1, cols), F32),
                jax.ShapeDtypeStruct((traits, traits), F32),
            ),
            in_specs=[anywhere] * 6,
            out_specs=(vmem, vmem, vmem),
            scratch_shapes=[
                pltpu.VMEM((nm, traits, mb), BF16),
                pltpu.VMEM((nb, traits, wb), BF16),
                pltpu.VMEM((nm * mb, traits), BF16),
                pltpu.VMEM((nb, nm * mb, wb), BF16),
                pltpu.VMEM((nb, traits, wb), F32),
                pltpu.VMEM((nb, wb), F32),
                pltpu.VMEM((nm * mb, wb if wb % 128 else 128), F32),
                pltpu.VMEM((xs, 1, rows), F32),
                pltpu.VMEM((traits, traits), F32),
                pltpu.VMEM((traits, traits), F32),
                pltpu.VMEM((1, cols), F32),
                pltpu.VMEM((xs, 1, rows), F32),
                pltpu.VMEM((xs, nb, wb), F32),
                pltpu.VMEM((2, nm, 1, nm * mb), F32),
                pltpu.VMEM((2, nb, nb, wb), F32),
                pltpu.VMEM((nm,) + packed, F32),
                pltpu.VMEM((cs,) + packed, F32),
                pltpu.VMEM((zs,) + packed, F32),
                dma((6,)),
                dma((nm,)), dma((nm,)),
                dma((zs,)), dma((zs,)),
                dma((zs,)), dma((zs,)),
                dma((xs,)), dma((xs,)),
                dma((xs,)), dma((xs,)),
                dma((3, nm)), dma((3, nm)),
                dma((2, nb)), dma((2, nb)),
                dma((cs,)), dma((cs,)),
                dma((zs,)), dma((zs,)),
            ],
            compiler_params=pltpu.CompilerParams(
                collective_id=0, has_side_effects=True, vmem_limit_bytes=60 * 1024 * 1024),
        )(men_traits, women_traits, affinity, observed,
          men_mass.reshape(1, rows), women_mass.reshape(1, cols))
        return out[0].reshape(rows), out[1].reshape(cols), out[2]

    placed = (P(None, ("men", "women")), P(None, ("women", "men")), P(), P(), P("men"), P("women"))
    return jax.shard_map(
        on_device,
        mesh=mesh,
        in_specs=placed,
        out_specs=(P("men"), P("women"), P()),
        check_vma=False,
    )
```
